256 devices in a mesh: row: 8 (over y, x_lo), col: 32 (over z, x_hi, core).
Axes of the slice: x: 4 (x_hi: 2, x_lo: 2; x = x_hi * 2 + x_lo), y: 4, z: 8, core: 2. Of those that a mesh axis runs over, the one named last changes fastest.
Arguments:
- grad_out: bfloat16 [3072, 8192], P('row', 'col'), may hold values from -6 to 6
- gate_act: bfloat16 [3072, 28672], P('row', 'col'), may hold values from -6 to 6
- up_act: bfloat16 [3072, 28672], P('row', 'col'), may hold values from -6 to 6
- down_weight: bfloat16 [28672, 8192], P('col', 'row'), may hold values from -0.0625 to 0.0625
Outputs:
- grad_gate: bfloat16 [3072, 28672], P('row', 'col')
- grad_up: bfloat16 [3072, 28672], P('row', 'col')
- grad_weight: float32 [28672, 8192], P('col', 'row')
The draws below stay inside these ranges and needn't reach their ends.
All inputs are finite; a program needn't handle non-finite values.
Results may differ from the reference program's by a relative error of at most 0.0028.
Values may be sent and summed in bfloat16 or wider, within the bound.
A program may use at most 128 MiB of HBM per device.

```python
import jax
import jax.numpy as jnp

D = 8192
FF = 28672
TOKENS = 3072


def levels(key, extent, cuts, low, top_value):
    level, own = 1.0, jax.random.fold_in(key, 6)
    for axis_at, parts in cuts:
        steps = jnp.exp(jax.random.uniform(jax.random.fold_in(own, axis_at), (parts,), jnp.float32, low / len(cuts), top_value / len(cuts)))
        level = level * jnp.repeat(steps, extent[axis_at] // parts).reshape([-1 if axis == axis_at else 1 for axis in range(len(extent))])
    return level


def centred(stream_key, dims, deviation, reach, shards=(), kind=jnp.bfloat16):
    loudness = levels(stream_key, dims, shards, -0.22, 0.18) if shards else 1.0
    entries = jax.random.normal(stream_key, dims, jnp.float32) * deviation * loudness
    return jnp.minimum(jnp.maximum(entries, -reach), reach).astype(kind)


def setup_inputs(seed: int = 0) -> dict:
    arg_keys = jax.random.split(jax.random.key(seed), 5)
    grad_out = centred(arg_keys[0], (TOKENS, D), 1.0, 6.0, ((0, 8), (1, 32)))
    gate_act = centred(arg_keys[1], (TOKENS, FF), 1.5, 6.0, ((0, 8), (1, 32)))
    up_act = centred(arg_keys[2], (TOKENS, FF), 1.0, 6.0, ((0, 8), (1, 32)))
    down_weight = centred(arg_keys[3], (FF, D), D ** -0.5, 0.0625, ((0, 32), (1, 8)))
    return dict(grad_out=grad_out, gate_act=gate_act, up_act=up_act, down_weight=down_weight)


def reference(grad_out, gate_act, up_act, down_weight):
    grad_hidden = jnp.dot(grad_out, down_weight.T, preferred_element_type=jnp.float32)
    gate_value = gate_act.astype(jnp.float32)
    up_value = up_act.astype(jnp.float32)
    sigmoid_gate = jax.nn.sigmoid(gate_value)
    swish = gate_value * sigmoid_gate
    grad_gate = (grad_hidden * up_value * sigmoid_gate * (1.0 + gate_value * (1.0 - sigmoid_gate))).astype(jnp.bfloat16)
    grad_up = (grad_hidden * swish).astype(jnp.bfloat16)
    hidden = (swish * up_value).astype(jnp.bfloat16)
    grad_weight = jnp.dot(hidden.T, grad_out, preferred_element_type=jnp.float32)
    return grad_gate, grad_up, grad_weight
```

```python
import jax
import jax.numpy as jnp
from jax import lax
from jax.experimental import pallas as pl
from jax.experimental.pallas import tpu as pltpu
from jax.sharding import PartitionSpec as P

MESH = pl.DeviceIdType.MESH
TB = 384
FB = 896
DR = 1024
DC = 256
CH = 4
NQ = 4 * CH
ROWS = TB // CH
HOPS = 7
SKEW = 2
F_TILES = ((0, 256), (256, 256), (512, 256), (768, 128))


def place(j):
    return j + lax.div(j, 2) - 2 * lax.div(j, 3)


ORDER = (0, 1, 3, 2)


def kernel(
    g_hbm, ga_hbm, up_hbm, w_hbm, gg_hbm, gu_hbm, gw_hbm,
    g1, g2, w2, ht, part, got, acc, ga, up, ggv, guv, gwv,
    loc_sem, out_sem,
    send_a, recv_a, send_w, recv_w, send_h, recv_h, send_r, recv_r,
    send_z, recv_z, send_s, recv_s, send_o, recv_o, send_p, recv_p,
):
    r = lax.axis_index("row")
    c = lax.axis_index("col")
    y, xl = lax.div(r, 2), lax.rem(r, 2)
    z = lax.div(c, 4)
    xh = lax.rem(lax.div(c, 2), 2)
    k = lax.rem(c, 2)
    sib = (r, c + 1 - 2 * k)
    partner = (r + 1 - 2 * xl, c)
    outer = (r + 1 - 2 * xl, c + 2 - 4 * xh)
    c2 = c + 2 - 4 * xh

    def ring_y(o):
        return lax.rem(r + 2 * o, 8)

    z_next = (
        (r, lax.rem(c + 4, 32)),
        (r, lax.rem(c + 28, 32)),
    )

    def remote(src, dst, ssem, rsem, dev):
        return pltpu.make_async_remote_copy(
            src_ref=src, dst_ref=dst, send_sem=ssem, recv_sem=rsem,
            device_id=dev, device_id_type=MESH,
        )

    def arrived(ref, sem):
        pltpu.make_async_copy(ref, ref, sem).wait()

    load_ga = pltpu.make_async_copy(ga_hbm, ga, loc_sem.at[0])
    load_up = pltpu.make_async_copy(up_hbm, up, loc_sem.at[1])
    load_w = pltpu.make_async_copy(w_hbm, w2.at[xl], loc_sem.at[2])
    load_ga.start()
    load_up.start()
    load_w.start()

    barrier = pltpu.get_barrier_semaphore()
    peers = [(ring_y(o), c) for o in (1, 2, 3)]
    peers += [(ring_y(o), c2) for o in (0, 1, 2, 3)]
    peers += [sib, partner, outer, z_next[0], z_next[1]]
    for dev in peers:
        pl.semaphore_signal(barrier, inc=1, device_id=dev, device_id_type=MESH)

    load_ga.wait()
    load_up.wait()

    def hidden_tile(i, carry):
        cols = pl.ds(pl.multiple_of(i * 128, 128), 128)
        gv = ga[:, cols].astype(jnp.float32)
        uv = up[:, cols].astype(jnp.float32)
        hv = gv * jax.nn.sigmoid(gv) * uv
        ht[r, cols, :] = hv.T.astype(jnp.bfloat16)
        return carry

    lax.fori_loop(0, FB // 128, hidden_tile, 0)

    pl.semaphore_wait(barrier, len(peers))

    yr = lax.div(z, 2)
    zb_own = lax.rem(z, 2)
    unit_cols = pl.ds(pl.multiple_of((2 * xh + k) * DC, DC), DC)
    a_dst = g1.at[zb_own, y, :, unit_cols]
    root_row = 2 * yr + xl
    a_slot = y * 2 + xh
    a_far = remote(g_hbm, a_dst, send_a.at[1], recv_a.at[a_slot], (root_row, c2))
    a_near = remote(g_hbm, a_dst, send_a.at[0], recv_a.at[a_slot], (root_row, c))
    a_local = pltpu.make_async_copy(g_hbm, a_dst, recv_a.at[a_slot])

    @pl.when(yr == y)
    def _():
        a_local.start()

    @pl.when(yr != y)
    def _():
        a_near.start()

    a_far.start()

    def hidden_sends(slot, base, devs):
        out = []
        for i, dev in enumerate(devs):
            out.append(
                remote(ht.at[slot], ht.at[slot], send_h.at[base + i], recv_h.at[slot], dev)
            )
        return out

    y_devs = [(ring_y(o), c) for o in (1, 3, 2)]
    own_h = hidden_sends(r, 0, y_devs + [partner])
    for d in own_h[:3]:
        d.start()

    w_sends = []
    for i, (f0, fn) in enumerate(F_TILES):
        w_sends.append(
            remote(
                w_hbm.at[pl.ds(f0, fn), :], w2.at[xl, pl.ds(f0, fn), :],
                send_w.at[i], recv_w.at[i], partner,
            )
        )
    w_sends[0].start()
    own_h[3].start()
    for d in w_sends[1:]:
        d.start()

    def lane_distance(zb, way):
        root = 2 * y + zb
        if way == 0:
            return lax.rem(z - root + 8, 8)
        return lax.rem(root - z + 8, 8)

    def lane_cols(way):
        return pl.ds(pl.multiple_of((2 * way + k) * DC, DC), DC)

    def block_of(j):
        return lax.rem(y + place(j), 4)

    def z_step(s, carry):
        for zb in range(2):
            for way in range(2):
                lane = 2 * zb + way
                d = lane_distance(zb, way)
                q = s - d

                @pl.when(jnp.logical_and(q >= 0, q < NQ))
                def _(zb=zb, way=way, lane=lane, d=d, q=q):
                    j = lax.div(q, CH)
                    p = lax.rem(q, CH)
                    yb = block_of(j)
                    rows = pl.ds(pl.multiple_of(p * ROWS, ROWS), ROWS)
                    ref = g1.at[zb, yb, rows, lane_cols(way)]

                    @pl.when(jnp.logical_and(d == 0, p == 0))
                    def _():
                        arrived(g1.at[zb, yb, :, lane_cols(way)], recv_a.at[yb * 2 + way])

                    @pl.when(d != 0)
                    def _():
                        arrived(ref, recv_z.at[lane * NQ + q])

                    @pl.when(d < HOPS)
                    def _():
                        remote(
                            ref, ref, send_z.at[lane], recv_z.at[lane * NQ + q], z_next[way]
                        ).start()

                    remote(ref, ref, send_s.at[lane], recv_s.at[lane * 4 + j], sib).start()

                    @pl.when(xl == 1 - zb)
                    def _():
                        remote(
                            ref, g2.at[yb, rows, lane_cols(way)],
                            send_o.at[way], recv_o.at[way * NQ + q], outer,
                        ).start()

        for way in range(2):
            d = jnp.where(xl == 0, lane_distance(0, way), lane_distance(1, way))
            q = s - SKEW - d

            @pl.when(jnp.logical_and(q >= 0, q < NQ))
            def _(way=way, q=q):
                j = lax.div(q, CH)
                p = lax.rem(q, CH)
                yb = block_of(j)
                rows = pl.ds(pl.multiple_of(p * ROWS, ROWS), ROWS)
                ref = g2.at[yb, rows, lane_cols(way)]
                arrived(ref, recv_o.at[way * NQ + q])
                remote(ref, ref, send_p.at[way], recv_p.at[way * 4 + j], sib).start()

        return carry

    half = NQ // 2
    last = NQ + HOPS + SKEW
    lax.fori_loop(0, half, z_step, 0)

    slot_p = r + 1 - 2 * xl
    arrived(ht.at[slot_p], recv_h.at[slot_p])
    fwd_h = hidden_sends(slot_p, 4, y_devs)
    for d in fwd_h:
        d.start()

    lax.fori_loop(half, last, z_step, 0)

    load_w.wait()
    for i, (f0, fn) in enumerate(F_TILES):
        arrived(w2.at[1 - xl, pl.ds(f0, fn), :], recv_w.at[i])

    nt = (((1,), (1,)), ((), ()))

    def product(yb, f0, fn):
        total = None
        for zb in range(2):
            term = lax.dot_general(
                g1[zb, yb], w2[zb, pl.ds(f0, fn), :], nt, preferred_element_type=jnp.float32
            )
            total = term if total is None else total + term
        return total

    r_sends = []
    for j in range(1, 4):
        o = ORDER[j]
        yb = lax.rem(y + o, 4)
        for zb in range(2):
            for way in range(2):
                lane = 2 * zb + way
                cols = pl.ds(pl.multiple_of((2 * way + 1 - k) * DC, DC), DC)
                arrived(g1.at[zb, yb, :, cols], recv_s.at[lane * 4 + j])
        for f0, fn in F_TILES:
            part[o - 1, :, f0 : f0 + fn] = product(yb, f0, fn).astype(jnp.bfloat16)
        send = remote(
            part.at[o - 1], got.at[o - 1], send_r.at[o - 1], recv_r.at[o - 1], (ring_y(o), c)
        )
        send.start()
        r_sends.append(send)

    for zb in range(2):
        for way in range(2):
            lane = 2 * zb + way
            cols = pl.ds(pl.multiple_of((2 * way + 1 - k) * DC, DC), DC)
            arrived(g1.at[zb, y, :, cols], recv_s.at[lane * 4])
    for f0, fn in F_TILES:
        acc[:, f0 : f0 + fn] = product(y, f0, fn)

    for way in range(2):
        cols = pl.ds(pl.multiple_of((2 * way + 1 - k) * DC, DC), DC)
        for j in range(4):
            yb = lax.rem(y + ORDER[j], 4)
            arrived(g2.at[yb, :, cols], recv_p.at[way * 4 + j])
    for o in (1, 3, 2):
        slot = ring_y(o)
        arrived(ht.at[slot], recv_h.at[slot])
    for o in (1, 3, 2):
        slot = lax.rem(slot_p + 2 * o, 8)
        arrived(ht.at[slot], recv_h.at[slot])

    def weight_tile(i, carry):
        cols = pl.ds(pl.multiple_of(i * 256, 256), 256)
        total = None
        for yb in range(4):
            for src, slot in ((g1.at[xl], 2 * yb + xl), (g2, 2 * yb + 1 - xl)):
                term = jnp.dot(
                    ht[slot], src[yb, :, cols], preferred_element_type=jnp.float32
                )
                total = term if total is None else total + term
        gwv[:, cols] = total
        pltpu.make_async_copy(gwv.at[:, cols], gw_hbm.at[:, cols], out_sem.at[2]).start()
        return carry

    lax.fori_loop(0, DR // 256, weight_tile, 0)

    for i in range(3):
        arrived(got.at[i], recv_r.at[i])

    def final_tile(i, carry):
        rows = pl.ds(pl.multiple_of(i * 32, 32), 32)
        gv = ga[rows, :].astype(jnp.float32)
        uv = up[rows, :].astype(jnp.float32)
        gh = acc[rows, :]
        for n in range(3):
            gh = gh + got[n, rows, :].astype(jnp.float32)
        s = jax.nn.sigmoid(gv)
        ggv[rows, :] = (gh * uv * s * (1.0 + gv * (1.0 - s))).astype(jnp.bfloat16)
        guv[rows, :] = (gh * (gv * s)).astype(jnp.bfloat16)
        return carry

    lax.fori_loop(0, TB // 32, final_tile, 0)
    out_gg = pltpu.make_async_copy(ggv, gg_hbm, out_sem.at[0])
    out_gu = pltpu.make_async_copy(guv, gu_hbm, out_sem.at[1])
    out_gg.start()
    out_gu.start()

    @pl.when(yr != y)
    def _():
        a_near.wait_send()

    a_far.wait_send()
    for d in own_h + fwd_h + w_sends + r_sends:
        d.wait_send()
    for zb in range(2):
        for way in range(2):
            lane = 2 * zb + way
            whole = g1.at[zb, :, :, lane_cols(way)]

            @pl.when(lane_distance(zb, way) < HOPS)
            def _(whole=whole, lane=lane):
                arrived(whole, send_z.at[lane])

            arrived(whole, send_s.at[lane])
    for way in range(2):
        whole = g2.at[:, :, lane_cols(way)]
        arrived(whole, send_o.at[way])
        arrived(whole, send_p.at[way])
    pltpu.make_async_copy(gwv, gw_hbm, out_sem.at[2]).wait()
    out_gg.wait()
    out_gu.wait()


def on_device(grad_out, gate_act, up_act, down_weight):
    bf, f32 = jnp.bfloat16, jnp.float32
    dma = pltpu.SemaphoreType.DMA
    hbm = pl.BlockSpec(memory_space=pl.ANY)
    return pl.pallas_call(
        kernel,
        out_shape=(
            jax.ShapeDtypeStruct((TB, FB), bf),
            jax.ShapeDtypeStruct((TB, FB), bf),
            jax.ShapeDtypeStruct((FB, DR), f32),
        ),
        in_specs=[hbm] * 4,
        out_specs=(hbm, hbm, hbm),
        scratch_shapes=[
            pltpu.VMEM((2, 4, TB, DR), bf),
            pltpu.VMEM((4, TB, DR), bf),
            pltpu.VMEM((2, FB, DR), bf),
            pltpu.VMEM((8, FB, TB), bf),
            pltpu.VMEM((3, TB, FB), bf),
            pltpu.VMEM((3, TB, FB), bf),
            pltpu.VMEM((TB, FB), f32),
            pltpu.VMEM((TB, FB), bf),
            pltpu.VMEM((TB, FB), bf),
            pltpu.VMEM((TB, FB), bf),
            pltpu.VMEM((TB, FB), bf),
            pltpu.VMEM((FB, DR), f32),
            dma((3,)), dma((3,)),
            dma((2,)), dma((8,)), dma((4,)), dma((4,)), dma((7,)), dma((8,)),
            dma((3,)), dma((3,)),
            dma((4,)), dma((4 * NQ,)), dma((4,)), dma((16,)),
            dma((2,)), dma((2 * NQ,)), dma((2,)), dma((8,)),
        ],
        compiler_params=pltpu.CompilerParams(
            collective_id=0, has_side_effects=True, vmem_limit_bytes=60 * 1024 * 1024
        ),
    )(grad_out, gate_act, up_act, down_weight)


def solution(mesh):
    placed = (P("row", "col"), P("row", "col"), P("row", "col"), P("col", "row"))
    return jax.shard_map(
        on_device,
        mesh=mesh,
        in_specs=placed,
        out_specs=(P("row", "col"), P("row", "col"), P("col", "row")),
        check_vma=False,
    )
```

```python
import functools

import jax
import jax.numpy as jnp
from jax import lax
from jax.experimental import pallas as pl
from jax.experimental.pallas import tpu as pltpu
from jax.sharding import PartitionSpec as P

MESH = pl.DeviceIdType.MESH
TB = 384
FB = 896
DR = 1024
DC = 256
CH = 8
NQ = 4 * CH
AP = CH // 2
AROWS = TB // AP
ROWS = TB // CH
HOPS = 7
W_AT = (25, 33, 42, 48)
AT_PASS, AT_OWN, AT_PARTNER = 18, 24, 37
LATER = 3
SKEW = 3
F_TILES = ((0, 256), (256, 256), (512, 256), (768, 128))


ORDER = ((0, 0), (0, 1), (2, 0), (2, 1), (1, 0), (3, 0), (1, 1), (3, 1))
HALF = TB // 2
FIRST = 2
HQ = CH // 2


def offset_of(h):
    return jnp.where(h < 2, 0, jnp.where(h < 4, 2, 1 + 2 * lax.rem(h, 2)))


def half_of(h):
    m = lax.div(h, 2)
    return jnp.where(m < 2, lax.rem(h, 2), m - 2)


UP = (0, 384)
DOWN = (384, 512)


def kernel(
    g_hbm, ga_hbm, up_hbm, w_hbm, ggv, guv, gwv,
    g1, g2, w2, ht, part, got, acc, ga, up,
    loc_sem,
    send_a, recv_a, send_w, recv_w, send_h, recv_h, recv_u, recv_d,
    send_r, recv_r,
    send_z, recv_z, send_s, recv_s, send_o, recv_o, send_p, recv_p,
):
    r = lax.axis_index("row")
    c = lax.axis_index("col")
    y, xl = lax.div(r, 2), lax.rem(r, 2)
    z = lax.div(c, 4)
    xh = lax.rem(lax.div(c, 2), 2)
    k = lax.rem(c, 2)
    sib = (r, c + 1 - 2 * k)
    partner = (r + 1 - 2 * xl, c)
    outer = (r + 1 - 2 * xl, c + 2 - 4 * xh)
    c2 = c + 2 - 4 * xh

    def ring_y(o):
        return lax.rem(r + 2 * o, 8)

    z_next = (
        (r, lax.rem(c + 4, 32)),
        (r, lax.rem(c + 28, 32)),
    )

    def remote(src, dst, ssem, rsem, dev):
        return pltpu.make_async_remote_copy(
            src_ref=src, dst_ref=dst, send_sem=ssem, recv_sem=rsem,
            device_id=dev, device_id_type=MESH,
        )

    def arrived(ref, sem):
        pltpu.make_async_copy(ref, ref, sem).wait()

    load_ga = pltpu.make_async_copy(ga_hbm, ga, loc_sem.at[0])
    load_up = pltpu.make_async_copy(up_hbm, up, loc_sem.at[1])
    load_w = pltpu.make_async_copy(w_hbm, w2.at[xl], loc_sem.at[2])
    load_ga.start()
    load_up.start()
    load_w.start()

    barrier = pltpu.get_barrier_semaphore()
    peers = [(ring_y(o), c) for o in (1, 2, 3)]
    peers += [(ring_y(o), c2) for o in (0, 1, 2, 3)]
    peers += [sib, partner, outer, z_next[0], z_next[1]]
    for dev in peers:
        pl.semaphore_signal(barrier, inc=1, device_id=dev, device_id_type=MESH)

    pl.semaphore_wait(barrier, len(peers))

    yr = lax.div(z, 2)
    zb_own = lax.rem(z, 2)
    unit_cols = pl.ds(pl.multiple_of((2 * xh + k) * DC, DC), DC)
    root_row = 2 * yr + xl
    for p in range(AP):
        rows = pl.ds(p * AROWS, AROWS)
        src, dst = g_hbm.at[rows, :], g1.at[zb_own, y, rows, unit_cols]
        rsem = recv_a.at[(y * 2 + xh) * AP + p]
        remote(src, dst, send_a.at[1], rsem, (root_row, c2)).start()

        @pl.when(yr == y)
        def _(src=src, dst=dst, rsem=rsem):
            pltpu.make_async_copy(src, dst, rsem).start()

        @pl.when(yr != y)
        def _(src=src, dst=dst, rsem=rsem):
            remote(src, dst, send_a.at[0], rsem, (root_row, c)).start()

    load_ga.wait()
    load_up.wait()

    def hidden_tile(i, carry):
        cols = pl.ds(pl.multiple_of(i * 128, 128), 128)
        gv = ga[:, cols].astype(jnp.float32)
        uv = up[:, cols].astype(jnp.float32)
        hv = gv * jax.nn.sigmoid(gv) * uv
        ht[r, cols, :] = hv.T.astype(jnp.bfloat16)
        return carry

    lax.fori_loop(0, FB // 128, hidden_tile, 0)

    h_sends = []

    def send_hidden(slot, rows, rsem, dev):
        ref = ht.at[slot, pl.ds(*rows), :]
        d = remote(ref, ref, send_h.at[len(h_sends)], rsem, dev)
        h_sends.append(d)
        d.start()

    y_up, y_down, y_far = [(ring_y(o), c) for o in (1, 3, 2)]

    def to_neighbours(slot):
        for dev in (y_up, y_down):
            send_hidden(slot, (0, FB), recv_h.at[slot], dev)

    def relay_hidden(kind, base):
        below, above = lax.rem(base + 6, 8), lax.rem(base + 2, 8)
        arrived(ht.at[below], recv_h.at[below])
        send_hidden(below, UP, recv_u.at[kind], y_up)
        arrived(ht.at[above], recv_h.at[above])
        send_hidden(above, DOWN, recv_d.at[kind], y_down)

    to_neighbours(r)
    send_hidden(r, (0, FB), recv_h.at[r], partner)

    w_sends = []
    for i, (f0, fn) in enumerate(F_TILES):
        w_sends.append(
            remote(
                w_hbm.at[pl.ds(f0, fn), :], w2.at[xl, pl.ds(f0, fn), :],
                send_w.at[i], recv_w.at[i], partner,
            )
        )
        w_sends[-1].start()

    def lane_distance(zb, way):
        root = 2 * y + zb
        if way == 0:
            return lax.rem(z - root + 8, 8)
        return lax.rem(root - z + 8, 8)

    def lane_cols(way):
        return pl.ds(pl.multiple_of((2 * way + k) * DC, DC), DC)

    def piece_of(q):
        h = lax.div(q, HQ)
        p = half_of(h) * HQ + lax.rem(q, HQ)
        rows = pl.ds(pl.multiple_of(p * ROWS, ROWS), ROWS)
        return h, lax.rem(y + offset_of(h), 4), p, rows

    def z_step(s, carry):
        for zb in range(2):
            for way in range(2):
                lane = 2 * zb + way
                d = lane_distance(zb, way)
                q = s - SKEW * d

                @pl.when(jnp.logical_and(q >= 0, q < NQ))
                def _(zb=zb, way=way, lane=lane, d=d, q=q):
                    h, yb, p, rows = piece_of(q)
                    ref = g1.at[zb, yb, rows, lane_cols(way)]

                    @pl.when(jnp.logical_and(d == 0, lax.rem(p, 2) == 0))
                    def _():
                        m = lax.div(p, 2)
                        piece = pl.ds(pl.multiple_of(m * AROWS, AROWS), AROWS)
                        arrived(
                            g1.at[zb, yb, piece, lane_cols(way)],
                            recv_a.at[(yb * 2 + way) * AP + m],
                        )

                    @pl.when(d != 0)
                    def _():
                        arrived(ref, recv_z.at[lane * NQ + q])

                    @pl.when(d < HOPS)
                    def _():
                        remote(
                            ref, ref, send_z.at[lane], recv_z.at[lane * NQ + q], z_next[way]
                        ).start()

                    remote(ref, ref, send_s.at[lane], recv_s.at[lane * 8 + h], sib).start()

                    @pl.when(xl == 1 - zb)
                    def _():
                        remote(
                            ref, g2.at[yb, rows, lane_cols(way)],
                            send_o.at[way], recv_o.at[way * NQ + q], outer,
                        ).start()

        for way in range(2):
            d = jnp.where(xl == 0, lane_distance(0, way), lane_distance(1, way))
            q = s - LATER - SKEW * d

            @pl.when(jnp.logical_and(q >= 0, q < NQ))
            def _(way=way, q=q):
                h, yb, p, rows = piece_of(q)
                ref = g2.at[yb, rows, lane_cols(way)]
                arrived(ref, recv_o.at[way * NQ + q])
                remote(ref, ref, send_p.at[way], recv_p.at[way * 8 + h], sib).start()

        return carry

    slot_p = r + 1 - 2 * xl
    nt = (((1,), (1,)), ((), ()))

    def product(yb, half, f0, fn):
        total = None
        for zb in range(2):
            term = lax.dot_general(
                g1[zb, yb, half * HALF : (half + 1) * HALF, :], w2[zb, pl.ds(f0, fn), :], nt,
                preferred_element_type=jnp.float32,
            )
            total = term if total is None else total + term
        return total

    def half_ready(h):
        o, half = ORDER[h]
        yb = lax.rem(y + o, 4)
        for zb in range(2):
            for way in range(2):
                lane = 2 * zb + way
                cols = pl.ds(pl.multiple_of((2 * way + 1 - k) * DC, DC), DC)
                ref = g1.at[zb, yb, pl.ds(half * HALF, HALF), cols]
                arrived(ref, recv_s.at[lane * 8 + h])

    def cell(h, t):
        o, half = ORDER[h]
        f0, fn = F_TILES[t]
        if t == 0:
            half_ready(h)
        if h == FIRST:
            arrived(w2.at[1 - xl, pl.ds(f0, fn), :], recv_w.at[t])
        rows = pl.ds(half * HALF, HALF)
        tile = product(lax.rem(y + o, 4), half, f0, fn)
        part[o - 1, half * HALF : (half + 1) * HALF, f0 : f0 + fn] = tile.astype(jnp.bfloat16)
        src = part.at[o - 1, rows, pl.ds(f0, fn)]
        dst = got.at[o - 1, rows, pl.ds(f0, fn)]
        rsem = recv_r.at[(2 * (o - 1) + half) * 4 + t]
        remote(src, dst, send_r.at[o - 1], rsem, (ring_y(o), c)).start()

    def pass_on():
        arrived(ht.at[slot_p], recv_h.at[slot_p])
        to_neighbours(slot_p)

    def opposite_hidden(kind, base):
        slot = lax.rem(base + 4, 8)
        arrived(ht.at[slot, pl.ds(*UP), :], recv_u.at[kind])
        arrived(ht.at[slot, pl.ds(*DOWN), :], recv_d.at[kind])

    def extra_ready(o):
        yb = lax.rem(y + o, 4)
        for h in range(8):
            if ORDER[h][0] == o:
                for way in range(2):
                    cols = pl.ds(pl.multiple_of((2 * way + 1 - k) * DC, DC), DC)
                    ref = g2.at[yb, pl.ds(ORDER[h][1] * HALF, HALF), cols]
                    arrived(ref, recv_p.at[way * 8 + h])

    def weight_pass(blocks, first=False, last=False):
        def tile(i, carry):
            cols = pl.ds(pl.multiple_of(i * 256, 256), 256)
            total = None if first else gwv[:, cols]
            for kind, o in blocks:
                yb = lax.rem(y + o, 4)
                left = ht[2 * yb + (xl if kind == 0 else 1 - xl)]
                right = g1[xl, yb, :, cols] if kind == 0 else g2[yb, :, cols]
                term = jnp.dot(left, right, preferred_element_type=jnp.float32)
                total = term if total is None else total + term
            gwv[:, cols] = total
            return carry

        lax.fori_loop(0, DR // 256, tile, 0)

    def own_weights():
        half_ready(0)
        half_ready(1)
        weight_pass([(0, 0)], first=True)

    def opposite_weights():
        opposite_hidden(0, r)
        weight_pass([(0, 2)])

    def extra_weights():
        extra_ready(0)
        weight_pass([(1, 0)])

    base = SKEW * HOPS
    ready = [base + HQ * (h + 1) for h in range(8)]
    events = [
        (AT_PASS, pass_on),
        (AT_OWN, lambda: relay_hidden(0, r)),
        (AT_PARTNER, lambda: relay_hidden(1, slot_p)),
        (ready[1] + 2, own_weights),
        (ready[2] + 3, extra_weights),
        (ready[4] + 3, opposite_weights),
    ]
    for h in range(FIRST, 8):
        for t in range(4):
            step = max(ready[h] + 1 + t // 2, W_AT[t])
            events.append((step, functools.partial(cell, h, t)))
    events.append((NQ + base + LATER, lambda: None))
    load_w.wait()
    at = 0
    for step, event in sorted(events, key=lambda e: e[0]):
        if step > at:
            lax.fori_loop(at, step, z_step, 0)
        event()
        at = step

    for half in range(2):
        for f0, fn in F_TILES:
            acc[half * HALF : (half + 1) * HALF, f0 : f0 + fn] = product(y, half, f0, fn)
    for o in range(1, 4):
        extra_ready(o)
    opposite_hidden(1, slot_p)
    weight_pass([(0, 1), (0, 3), (1, 1), (1, 2), (1, 3)], last=True)

    for i in range(3):
        for half in range(2):
            for t, (f0, fn) in enumerate(F_TILES):
                ref = got.at[i, pl.ds(half * HALF, HALF), pl.ds(f0, fn)]
                arrived(ref, recv_r.at[(2 * i + half) * 4 + t])

    def final_tile(i, carry):
        rows = pl.ds(pl.multiple_of(i * 32, 32), 32)
        gv = ga[rows, :].astype(jnp.float32)
        uv = up[rows, :].astype(jnp.float32)
        gh = acc[rows, :]
        for n in range(3):
            gh = gh + got[n, rows, :].astype(jnp.float32)
        s = jax.nn.sigmoid(gv)
        ggv[rows, :] = (gh * uv * s * (1.0 + gv * (1.0 - s))).astype(jnp.bfloat16)
        guv[rows, :] = (gh * (gv * s)).astype(jnp.bfloat16)
        return carry

    lax.fori_loop(0, TB // 32, final_tile, 0)
    @pl.when(yr != y)
    def _():
        arrived(g_hbm, send_a.at[0])

    arrived(g_hbm, send_a.at[1])
    for d in h_sends + w_sends:
        d.wait_send()
    for i in range(3):
        arrived(part.at[i], send_r.at[i])
    for zb in range(2):
        for way in range(2):
            lane = 2 * zb + way
            whole = g1.at[zb, :, :, lane_cols(way)]

            @pl.when(lane_distance(zb, way) < HOPS)
            def _(whole=whole, lane=lane):
                arrived(whole, send_z.at[lane])

            arrived(whole, send_s.at[lane])
    for way in range(2):
        whole = g2.at[:, :, lane_cols(way)]
        arrived(whole, send_o.at[way])
        arrived(whole, send_p.at[way])


def on_device(grad_out, gate_act, up_act, down_weight):
    bf, f32 = jnp.bfloat16, jnp.float32
    dma = pltpu.SemaphoreType.DMA
    hbm = pl.BlockSpec(memory_space=pl.ANY)
    return pl.pallas_call(
        kernel,
        out_shape=(
            pltpu.VMEM((TB, FB), bf),
            pltpu.VMEM((TB, FB), bf),
            pltpu.VMEM((FB, DR), f32),
        ),
        in_specs=[hbm] * 4,
        out_specs=(pl.BlockSpec(memory_space=pltpu.VMEM),) * 3,
        scratch_shapes=[
            pltpu.VMEM((2, 4, TB, DR), bf),
            pltpu.VMEM((4, TB, DR), bf),
            pltpu.VMEM((2, FB, DR), bf),
            pltpu.VMEM((8, FB, TB), bf),
            pltpu.VMEM((3, TB, FB), bf),
            pltpu.VMEM((3, TB, FB), bf),
            pltpu.VMEM((TB, FB), f32),
            pltpu.VMEM((TB, FB), bf),
            pltpu.VMEM((TB, FB), bf),
            dma((3,)),
            dma((2,)), dma((8 * AP,)), dma((4,)), dma((4,)), dma((9,)), dma((8,)), dma((2,)), dma((2,)),
            dma((3,)), dma((24,)),
            dma((4,)), dma((4 * NQ,)), dma((4,)), dma((32,)),
            dma((2,)), dma((2 * NQ,)), dma((2,)), dma((16,)),
        ],
        compiler_params=pltpu.CompilerParams(
            collective_id=0, has_side_effects=True, vmem_limit_bytes=46 * 1024 * 1024
        ),
    )(grad_out, gate_act, up_act, down_weight)


def solution(mesh):
    placed = (P("row", "col"), P("row", "col"), P("row", "col"), P("col", "row"))
    return jax.shard_map(
        on_device,
        mesh=mesh,
        in_specs=placed,
        out_specs=(P("row", "col"), P("row", "col"), P("col", "row")),
        check_vma=False,
    )
```

```python
import functools

import jax
import jax.numpy as jnp
from jax import lax
from jax.experimental import pallas as pl
from jax.experimental.pallas import tpu as pltpu
from jax.sharding import PartitionSpec as P

MESH = pl.DeviceIdType.MESH
TB = 384
FB = 896
DR = 1024
DC = 256
CH = 8
NQ = 4 * CH
AP = CH // 2
AROWS = TB // AP
ROWS = TB // CH
HOPS = 7
W_AT = (25, 33, 42, 48)
AT_PASS, AT_OWN, AT_PARTNER = 18, 24, 37
LATER = 3
SKEW = 3
F_TILES = ((0, 256), (256, 256), (512, 256), (768, 128))


ORDER = ((0, 0), (0, 1), (2, 0), (2, 1), (1, 0), (3, 0), (1, 1), (3, 1))
HALF = TB // 2
FIRST = 2
HQ = CH // 2


def offset_of(h):
    return jnp.where(h < 2, 0, jnp.where(h < 4, 2, 1 + 2 * lax.rem(h, 2)))


def half_of(h):
    m = lax.div(h, 2)
    return jnp.where(m < 2, lax.rem(h, 2), m - 2)


UP = (0, 384)
DOWN = (384, 512)
OVER_Y = 512
UP2, DOWN2 = (0, 256), (256, 256)
OVER_X = (OVER_Y, FB - OVER_Y)


def kernel(
    g_hbm, ga_hbm, up_hbm, w_hbm, ggv, guv, gwv,
    g1, g2, w2, ht, part, got, acc, ga, up,
    loc_sem,
    send_a, recv_a, send_w, recv_w, send_h, recv_h, recv_u, recv_d, recv_x,
    send_r, recv_r,
    send_z, recv_z, send_s, recv_s, send_o, recv_o, send_p, recv_p,
):
    r = lax.axis_index("row")
    c = lax.axis_index("col")
    y, xl = lax.div(r, 2), lax.rem(r, 2)
    z = lax.div(c, 4)
    xh = lax.rem(lax.div(c, 2), 2)
    k = lax.rem(c, 2)
    sib = (r, c + 1 - 2 * k)
    partner = (r + 1 - 2 * xl, c)
    outer = (r + 1 - 2 * xl, c + 2 - 4 * xh)
    c2 = c + 2 - 4 * xh

    def ring_y(o):
        return lax.rem(r + 2 * o, 8)

    z_next = (
        (r, lax.rem(c + 4, 32)),
        (r, lax.rem(c + 28, 32)),
    )

    def remote(src, dst, ssem, rsem, dev):
        return pltpu.make_async_remote_copy(
            src_ref=src, dst_ref=dst, send_sem=ssem, recv_sem=rsem,
            device_id=dev, device_id_type=MESH,
        )

    def arrived(ref, sem):
        pltpu.make_async_copy(ref, ref, sem).wait()

    load_ga = pltpu.make_async_copy(ga_hbm, ga, loc_sem.at[0])
    load_up = pltpu.make_async_copy(up_hbm, up, loc_sem.at[1])
    load_w = pltpu.make_async_copy(w_hbm, w2.at[xl], loc_sem.at[2])
    load_ga.start()
    load_up.start()
    load_w.start()

    barrier = pltpu.get_barrier_semaphore()
    peers = [(ring_y(o), c) for o in (1, 2, 3)]
    peers += [(ring_y(o), c2) for o in (0, 1, 2, 3)]
    peers += [sib, partner, outer, z_next[0], z_next[1]]
    for dev in peers:
        pl.semaphore_signal(barrier, inc=1, device_id=dev, device_id_type=MESH)

    load_ga.wait()
    load_up.wait()

    def hidden_tile(i, carry):
        cols = pl.ds(pl.multiple_of(i * 128, 128), 128)
        gv = ga[:, cols].astype(jnp.float32)
        uv = up[:, cols].astype(jnp.float32)
        hv = gv * jax.nn.sigmoid(gv) * uv
        ht[r, cols, :] = hv.T.astype(jnp.bfloat16)
        return carry

    lax.fori_loop(0, FB // 128, hidden_tile, 0)

    pl.semaphore_wait(barrier, len(peers))

    yr = lax.div(z, 2)
    zb_own = lax.rem(z, 2)
    unit_cols = pl.ds(pl.multiple_of((2 * xh + k) * DC, DC), DC)
    root_row = 2 * yr + xl
    for p in range(AP):
        rows = pl.ds(p * AROWS, AROWS)
        src, dst = g_hbm.at[rows, :], g1.at[zb_own, y, rows, unit_cols]
        rsem = recv_a.at[(y * 2 + xh) * AP + p]
        remote(src, dst, send_a.at[1], rsem, (root_row, c2)).start()

        @pl.when(yr == y)
        def _(src=src, dst=dst, rsem=rsem):
            pltpu.make_async_copy(src, dst, rsem).start()

        @pl.when(yr != y)
        def _(src=src, dst=dst, rsem=rsem):
            remote(src, dst, send_a.at[0], rsem, (root_row, c)).start()

    h_sends = []

    def send_hidden(slot, rows, rsem, dev):
        ref = ht.at[slot, pl.ds(*rows), :]
        d = remote(ref, ref, send_h.at[len(h_sends)], rsem, dev)
        h_sends.append(d)
        d.start()

    y_up, y_down, y_far = [(ring_y(o), c) for o in (1, 3, 2)]

    def to_neighbours(slot, rows):
        for dev in (y_up, y_down):
            send_hidden(slot, rows, recv_h.at[slot], dev)

    def over_x(slot, i):
        send_hidden(slot, OVER_X, recv_x.at[i], partner)

    def relay_hidden(kind, base):
        below, above = lax.rem(base + 6, 8), lax.rem(base + 2, 8)
        rows = pl.ds(0, (FB, OVER_Y)[kind])
        arrived(ht.at[below, rows, :], recv_h.at[below])
        send_hidden(below, (UP, UP2)[kind], recv_u.at[kind], y_up)
        arrived(ht.at[above, rows, :], recv_h.at[above])
        send_hidden(above, (DOWN, DOWN2)[kind], recv_d.at[kind], y_down)
        if kind == 0:
            over_x(below, 0)
            over_x(above, 1)

    to_neighbours(r, (0, FB))
    send_hidden(r, (0, FB), recv_h.at[r], partner)

    w_sends = []
    for i, (f0, fn) in enumerate(F_TILES):
        w_sends.append(
            remote(
                w_hbm.at[pl.ds(f0, fn), :], w2.at[xl, pl.ds(f0, fn), :],
                send_w.at[i], recv_w.at[i], partner,
            )
        )
        w_sends[-1].start()

    def lane_distance(zb, way):
        root = 2 * y + zb
        if way == 0:
            return lax.rem(z - root + 8, 8)
        return lax.rem(root - z + 8, 8)

    def lane_cols(way):
        return pl.ds(pl.multiple_of((2 * way + k) * DC, DC), DC)

    def piece_of(q):
        h = lax.div(q, HQ)
        p = half_of(h) * HQ + lax.rem(q, HQ)
        rows = pl.ds(pl.multiple_of(p * ROWS, ROWS), ROWS)
        return h, lax.rem(y + offset_of(h), 4), p, rows

    def z_step(s, carry):
        for zb in range(2):
            for way in range(2):
                lane = 2 * zb + way
                d = lane_distance(zb, way)
                q = s - SKEW * d

                @pl.when(jnp.logical_and(q >= 0, q < NQ))
                def _(zb=zb, way=way, lane=lane, d=d, q=q):
                    h, yb, p, rows = piece_of(q)
                    ref = g1.at[zb, yb, rows, lane_cols(way)]

                    @pl.when(jnp.logical_and(d == 0, lax.rem(p, 2) == 0))
                    def _():
                        m = lax.div(p, 2)
                        piece = pl.ds(pl.multiple_of(m * AROWS, AROWS), AROWS)
                        arrived(
                            g1.at[zb, yb, piece, lane_cols(way)],
                            recv_a.at[(yb * 2 + way) * AP + m],
                        )

                    @pl.when(d != 0)
                    def _():
                        arrived(ref, recv_z.at[lane * NQ + q])

                    @pl.when(d < HOPS)
                    def _():
                        remote(
                            ref, ref, send_z.at[lane], recv_z.at[lane * NQ + q], z_next[way]
                        ).start()

                    remote(ref, ref, send_s.at[lane], recv_s.at[lane * 8 + h], sib).start()

                    @pl.when(xl == 1 - zb)
                    def _():
                        remote(
                            ref, g2.at[yb, rows, lane_cols(way)],
                            send_o.at[way], recv_o.at[way * NQ + q], outer,
                        ).start()

        for way in range(2):
            d = jnp.where(xl == 0, lane_distance(0, way), lane_distance(1, way))
            q = s - LATER - SKEW * d

            @pl.when(jnp.logical_and(q >= 0, q < NQ))
            def _(way=way, q=q):
                h, yb, p, rows = piece_of(q)
                ref = g2.at[yb, rows, lane_cols(way)]
                arrived(ref, recv_o.at[way * NQ + q])
                remote(ref, ref, send_p.at[way], recv_p.at[way * 8 + h], sib).start()

        return carry

    slot_p = r + 1 - 2 * xl
    nt = (((1,), (1,)), ((), ()))

    def product(yb, half, f0, fn):
        total = None
        for zb in range(2):
            term = lax.dot_general(
                g1[zb, yb, half * HALF : (half + 1) * HALF, :], w2[zb, pl.ds(f0, fn), :], nt,
                preferred_element_type=jnp.float32,
            )
            total = term if total is None else total + term
        return total

    def half_ready(h):
        o, half = ORDER[h]
        yb = lax.rem(y + o, 4)
        for zb in range(2):
            for way in range(2):
                lane = 2 * zb + way
                cols = pl.ds(pl.multiple_of((2 * way + 1 - k) * DC, DC), DC)
                ref = g1.at[zb, yb, pl.ds(half * HALF, HALF), cols]
                arrived(ref, recv_s.at[lane * 8 + h])

    def cell(h, t):
        o, half = ORDER[h]
        f0, fn = F_TILES[t]
        if t == 0:
            half_ready(h)
        if h == FIRST:
            arrived(w2.at[1 - xl, pl.ds(f0, fn), :], recv_w.at[t])
        rows = pl.ds(half * HALF, HALF)
        tile = product(lax.rem(y + o, 4), half, f0, fn)
        part[o - 1, half * HALF : (half + 1) * HALF, f0 : f0 + fn] = tile.astype(jnp.bfloat16)
        src = part.at[o - 1, rows, pl.ds(f0, fn)]
        dst = got.at[o - 1, rows, pl.ds(f0, fn)]
        rsem = recv_r.at[(2 * (o - 1) + half) * 4 + t]
        remote(src, dst, send_r.at[o - 1], rsem, (ring_y(o), c)).start()

    def pass_on():
        arrived(ht.at[slot_p], recv_h.at[slot_p])
        to_neighbours(slot_p, (0, OVER_Y))

    def opposite_hidden(kind, base):
        slot = lax.rem(base + 4, 8)
        arrived(ht.at[slot, pl.ds(*(UP, UP2)[kind]), :], recv_u.at[kind])
        arrived(ht.at[slot, pl.ds(*(DOWN, DOWN2)[kind]), :], recv_d.at[kind])
        if kind == 0:
            over_x(slot, 2)

    def extra_ready(o):
        yb = lax.rem(y + o, 4)
        for h in range(8):
            if ORDER[h][0] == o:
                for way in range(2):
                    cols = pl.ds(pl.multiple_of((2 * way + 1 - k) * DC, DC), DC)
                    ref = g2.at[yb, pl.ds(ORDER[h][1] * HALF, HALF), cols]
                    arrived(ref, recv_p.at[way * 8 + h])

    def weight_pass(blocks, first=False, last=False):
        def tile(i, carry):
            cols = pl.ds(pl.multiple_of(i * 256, 256), 256)
            total = None if first else gwv[:, cols]
            for kind, o in blocks:
                yb = lax.rem(y + o, 4)
                left = ht[2 * yb + (xl if kind == 0 else 1 - xl)]
                right = g1[xl, yb, :, cols] if kind == 0 else g2[yb, :, cols]
                term = jnp.dot(left, right, preferred_element_type=jnp.float32)
                total = term if total is None else total + term
            gwv[:, cols] = total
            return carry

        lax.fori_loop(0, DR // 256, tile, 0)

    def own_weights():
        half_ready(0)
        half_ready(1)
        weight_pass([(0, 0)], first=True)

    def opposite_weights():
        opposite_hidden(0, r)
        weight_pass([(0, 2)])

    def extra_weights():
        extra_ready(0)
        weight_pass([(1, 0)])

    base = SKEW * HOPS
    ready = [base + HQ * (h + 1) for h in range(8)]
    events = [
        (AT_PASS, pass_on),
        (AT_OWN, lambda: relay_hidden(0, r)),
        (AT_PARTNER, lambda: relay_hidden(1, slot_p)),
        (ready[1] + 2, own_weights),
        (ready[2] + 3, extra_weights),
        (ready[4] + 3, opposite_weights),
    ]
    for h in range(FIRST, 8):
        for t in range(4):
            step = max(ready[h] + 1 + t // 2, W_AT[t])
            events.append((step, functools.partial(cell, h, t)))
    events.append((NQ + base + LATER, lambda: None))
    load_w.wait()
    at = 0
    for step, event in sorted(events, key=lambda e: e[0]):
        if step > at:
            lax.fori_loop(at, step, z_step, 0)
        event()
        at = step

    for half in range(2):
        for f0, fn in F_TILES:
            acc[half * HALF : (half + 1) * HALF, f0 : f0 + fn] = product(y, half, f0, fn)
    for o in range(1, 4):
        extra_ready(o)
    opposite_hidden(1, slot_p)
    for i, o in enumerate((3, 1, 2)):
        slot = lax.rem(slot_p + 2 * o, 8)
        arrived(ht.at[slot, pl.ds(*OVER_X), :], recv_x.at[i])
    weight_pass([(0, 1), (0, 3), (1, 1), (1, 2), (1, 3)], last=True)

    for i in range(3):
        for half in range(2):
            for t, (f0, fn) in enumerate(F_TILES):
                ref = got.at[i, pl.ds(half * HALF, HALF), pl.ds(f0, fn)]
                arrived(ref, recv_r.at[(2 * i + half) * 4 + t])

    def final_tile(i, carry):
        rows = pl.ds(pl.multiple_of(i * 32, 32), 32)
        gv = ga[rows, :].astype(jnp.float32)
        uv = up[rows, :].astype(jnp.float32)
        gh = acc[rows, :]
        for n in range(3):
            gh = gh + got[n, rows, :].astype(jnp.float32)
        s = jax.nn.sigmoid(gv)
        ggv[rows, :] = (gh * uv * s * (1.0 + gv * (1.0 - s))).astype(jnp.bfloat16)
        guv[rows, :] = (gh * (gv * s)).astype(jnp.bfloat16)
        return carry

    lax.fori_loop(0, TB // 32, final_tile, 0)
    @pl.when(yr != y)
    def _():
        arrived(g_hbm, send_a.at[0])

    arrived(g_hbm, send_a.at[1])
    for d in h_sends + w_sends:
        d.wait_send()
    for i in range(3):
        arrived(part.at[i], send_r.at[i])
    for zb in range(2):
        for way in range(2):
            lane = 2 * zb + way
            whole = g1.at[zb, :, :, lane_cols(way)]

            @pl.when(lane_distance(zb, way) < HOPS)
            def _(whole=whole, lane=lane):
                arrived(whole, send_z.at[lane])

            arrived(whole, send_s.at[lane])
    for way in range(2):
        whole = g2.at[:, :, lane_cols(way)]
        arrived(whole, send_o.at[way])
        arrived(whole, send_p.at[way])


def on_device(grad_out, gate_act, up_act, down_weight):
    bf, f32 = jnp.bfloat16, jnp.float32
    dma = pltpu.SemaphoreType.DMA
    hbm = pl.BlockSpec(memory_space=pltpu.HBM)
    return pl.pallas_call(
        kernel,
        out_shape=(
            pltpu.VMEM((TB, FB), bf),
            pltpu.VMEM((TB, FB), bf),
            pltpu.VMEM((FB, DR), f32),
        ),
        in_specs=[hbm] * 4,
        out_specs=(pl.BlockSpec(memory_space=pltpu.VMEM),) * 3,
        scratch_shapes=[
            pltpu.VMEM((2, 4, TB, DR), bf),
            pltpu.VMEM((4, TB, DR), bf),
            pltpu.VMEM((2, FB, DR), bf),
            pltpu.VMEM((8, FB, TB), bf),
            pltpu.VMEM((3, TB, FB), bf),
            pltpu.VMEM((3, TB, FB), bf),
            pltpu.VMEM((TB, FB), f32),
            pltpu.VMEM((TB, FB), bf),
            pltpu.VMEM((TB, FB), bf),
            dma((3,)),
            dma((2,)), dma((8 * AP,)), dma((4,)), dma((4,)), dma((12,)), dma((8,)), dma((2,)), dma((2,)), dma((3,)),
            dma((3,)), dma((24,)),
            dma((4,)), dma((4 * NQ,)), dma((4,)), dma((32,)),
            dma((2,)), dma((2 * NQ,)), dma((2,)), dma((16,)),
        ],
        compiler_params=pltpu.CompilerParams(
            collective_id=0, has_side_effects=True, vmem_limit_bytes=59 * 1024 * 1024
        ),
    )(grad_out, gate_act, up_act, down_weight)


def solution(mesh):
    placed = (P("row", "col"), P("row", "col"), P("row", "col"), P("col", "row"))
    return jax.shard_map(
        on_device,
        mesh=mesh,
        in_specs=placed,
        out_specs=(P("row", "col"), P("row", "col"), P("col", "row")),
        check_vma=False,
    )
```

```python
import functools

import jax
import jax.numpy as jnp
from jax import lax
from jax.experimental import pallas as pl
from jax.experimental.pallas import tpu as pltpu
from jax.sharding import PartitionSpec as P

MESH = pl.DeviceIdType.MESH
TB = 384
FB = 896
DR = 1024
DC = 256
CH = 8
NQ = 4 * CH
AP = CH // 2
AROWS = TB // AP
ROWS = TB // CH
HOPS = 7
W_AT = (25, 33, 42, 48)
AT_PASS, AT_OWN, AT_PARTNER = 18, 24, 37
LATER = 3
SKEW = 3
F_TILES = ((0, 256), (256, 256), (512, 256), (768, 128))


ORDER = ((0, 0), (0, 1), (2, 0), (2, 1), (1, 0), (3, 0), (1, 1), (3, 1))
HALF = TB // 2
FIRST = 2
HQ = CH // 2


def offset_of(h):
    return jnp.where(h < 2, 0, jnp.where(h < 4, 2, 1 + 2 * lax.rem(h, 2)))


def half_of(h):
    m = lax.div(h, 2)
    return jnp.where(m < 2, lax.rem(h, 2), m - 2)


UP = (0, 384)
DOWN = (384, 512)
OVER_Y = 512
UP2, DOWN2 = (0, 256), (256, 256)
OVER_X = (OVER_Y, FB - OVER_Y)


def kernel(
    g_hbm, ga_hbm, up_hbm, w_hbm, ggv, guv, gwv,
    g1, g2, w2, ht, part, got, acc, ga, up,
    loc_sem,
    send_a, recv_a, send_w, recv_w, send_h, recv_h, recv_u, recv_d, recv_x,
    send_r, recv_r,
    send_z, recv_z, send_s, recv_s, send_o, recv_o, send_p, recv_p,
):
    r = lax.axis_index("row")
    c = lax.axis_index("col")
    y, xl = lax.div(r, 2), lax.rem(r, 2)
    z = lax.div(c, 4)
    xh = lax.rem(lax.div(c, 2), 2)
    k = lax.rem(c, 2)
    sib = (r, c + 1 - 2 * k)
    partner = (r + 1 - 2 * xl, c)
    outer = (r + 1 - 2 * xl, c + 2 - 4 * xh)
    c2 = c + 2 - 4 * xh

    def ring_y(o):
        return lax.rem(r + 2 * o, 8)

    z_next = (
        (r, lax.rem(c + 4, 32)),
        (r, lax.rem(c + 28, 32)),
    )

    def remote(src, dst, ssem, rsem, dev):
        return pltpu.make_async_remote_copy(
            src_ref=src, dst_ref=dst, send_sem=ssem, recv_sem=rsem,
            device_id=dev, device_id_type=MESH,
        )

    def arrived(ref, sem):
        pltpu.make_async_copy(ref, ref, sem).wait()

    load_ga = pltpu.make_async_copy(ga_hbm, ga, loc_sem.at[0])
    load_up = pltpu.make_async_copy(up_hbm, up, loc_sem.at[1])
    load_w = pltpu.make_async_copy(w_hbm, w2.at[xl], loc_sem.at[2])
    load_ga.start()
    load_up.start()
    load_w.start()

    barrier = pltpu.get_barrier_semaphore()
    peers = [(ring_y(o), c) for o in (1, 2, 3)]
    peers += [(ring_y(o), c2) for o in (0, 1, 2, 3)]
    peers += [sib, partner, outer, z_next[0], z_next[1]]
    for dev in peers:
        pl.semaphore_signal(barrier, inc=1, device_id=dev, device_id_type=MESH)

    pl.semaphore_wait(barrier, len(peers))

    yr = lax.div(z, 2)
    zb_own = lax.rem(z, 2)
    unit_cols = pl.ds(pl.multiple_of((2 * xh + k) * DC, DC), DC)
    root_row = 2 * yr + xl
    for p in range(AP):
        rows = pl.ds(p * AROWS, AROWS)
        src, dst = g_hbm.at[rows, :], g1.at[zb_own, y, rows, unit_cols]
        rsem = recv_a.at[(y * 2 + xh) * AP + p]
        remote(src, dst, send_a.at[1], rsem, (root_row, c2)).start()

        @pl.when(yr == y)
        def _(src=src, dst=dst, rsem=rsem):
            pltpu.make_async_copy(src, dst, rsem).start()

        @pl.when(yr != y)
        def _(src=src, dst=dst, rsem=rsem):
            remote(src, dst, send_a.at[0], rsem, (root_row, c)).start()

    load_ga.wait()
    load_up.wait()

    def hidden_tile(i, carry):
        cols = pl.ds(pl.multiple_of(i * 128, 128), 128)
        gv = ga[:, cols].astype(jnp.float32)
        uv = up[:, cols].astype(jnp.float32)
        hv = gv * jax.nn.sigmoid(gv) * uv
        ht[r, cols, :] = hv.T.astype(jnp.bfloat16)
        return carry

    lax.fori_loop(0, FB // 128, hidden_tile, 0)

    h_sends = []

    def send_hidden(slot, rows, rsem, dev):
        ref = ht.at[slot, pl.ds(*rows), :]
        d = remote(ref, ref, send_h.at[len(h_sends)], rsem, dev)
        h_sends.append(d)
        d.start()

    y_up, y_down, y_far = [(ring_y(o), c) for o in (1, 3, 2)]

    def to_neighbours(slot, rows):
        for dev in (y_up, y_down):
            send_hidden(slot, rows, recv_h.at[slot], dev)

    def over_x(slot, i):
        send_hidden(slot, OVER_X, recv_x.at[i], partner)

    def relay_hidden(kind, base):
        below, above = lax.rem(base + 6, 8), lax.rem(base + 2, 8)
        rows = pl.ds(0, (FB, OVER_Y)[kind])
        arrived(ht.at[below, rows, :], recv_h.at[below])
        send_hidden(below, (UP, UP2)[kind], recv_u.at[kind], y_up)
        arrived(ht.at[above, rows, :], recv_h.at[above])
        send_hidden(above, (DOWN, DOWN2)[kind], recv_d.at[kind], y_down)
        if kind == 0:
            over_x(below, 0)
            over_x(above, 1)

    to_neighbours(r, (0, FB))
    send_hidden(r, (0, FB), recv_h.at[r], partner)

    w_sends = []
    for i, (f0, fn) in enumerate(F_TILES):
        w_sends.append(
            remote(
                w_hbm.at[pl.ds(f0, fn), :], w2.at[xl, pl.ds(f0, fn), :],
                send_w.at[i], recv_w.at[i], partner,
            )
        )
        w_sends[-1].start()

    def lane_distance(zb, way):
        root = 2 * y + zb
        if way == 0:
            return lax.rem(z - root + 8, 8)
        return lax.rem(root - z + 8, 8)

    def lane_cols(way):
        return pl.ds(pl.multiple_of((2 * way + k) * DC, DC), DC)

    def piece_of(q):
        h = lax.div(q, HQ)
        p = half_of(h) * HQ + lax.rem(q, HQ)
        rows = pl.ds(pl.multiple_of(p * ROWS, ROWS), ROWS)
        return h, lax.rem(y + offset_of(h), 4), p, rows

    def z_step(s, carry):
        for zb in range(2):
            for way in range(2):
                lane = 2 * zb + way
                d = lane_distance(zb, way)
                q = s - SKEW * d

                @pl.when(jnp.logical_and(q >= 0, q < NQ))
                def _(zb=zb, way=way, lane=lane, d=d, q=q):
                    h, yb, p, rows = piece_of(q)
                    ref = g1.at[zb, yb, rows, lane_cols(way)]

                    @pl.when(jnp.logical_and(d == 0, lax.rem(p, 2) == 0))
                    def _():
                        m = lax.div(p, 2)
                        piece = pl.ds(pl.multiple_of(m * AROWS, AROWS), AROWS)
                        arrived(
                            g1.at[zb, yb, piece, lane_cols(way)],
                            recv_a.at[(yb * 2 + way) * AP + m],
                        )

                    @pl.when(d != 0)
                    def _():
                        arrived(ref, recv_z.at[lane * NQ + q])

                    @pl.when(d < HOPS)
                    def _():
                        remote(
                            ref, ref, send_z.at[lane], recv_z.at[lane * NQ + q], z_next[way]
                        ).start()

                    remote(ref, ref, send_s.at[lane], recv_s.at[lane * 8 + h], sib).start()

                    @pl.when(xl == 1 - zb)
                    def _():
                        remote(
                            ref, g2.at[yb, rows, lane_cols(way)],
                            send_o.at[way], recv_o.at[way * NQ + q], outer,
                        ).start()

        for way in range(2):
            d = jnp.where(xl == 0, lane_distance(0, way), lane_distance(1, way))
            q = s - LATER - SKEW * d

            @pl.when(jnp.logical_and(q >= 0, q < NQ))
            def _(way=way, q=q):
                h, yb, p, rows = piece_of(q)
                ref = g2.at[yb, rows, lane_cols(way)]
                arrived(ref, recv_o.at[way * NQ + q])
                remote(ref, ref, send_p.at[way], recv_p.at[way * 8 + h], sib).start()

        return carry

    slot_p = r + 1 - 2 * xl
    nt = (((1,), (1,)), ((), ()))

    def product(yb, half, f0, fn):
        total = None
        for zb in range(2):
            term = lax.dot_general(
                g1[zb, yb, half * HALF : (half + 1) * HALF, :], w2[zb, pl.ds(f0, fn), :], nt,
                preferred_element_type=jnp.float32,
            )
            total = term if total is None else total + term
        return total

    def half_ready(h):
        o, half = ORDER[h]
        yb = lax.rem(y + o, 4)
        for zb in range(2):
            for way in range(2):
                lane = 2 * zb + way
                cols = pl.ds(pl.multiple_of((2 * way + 1 - k) * DC, DC), DC)
                ref = g1.at[zb, yb, pl.ds(half * HALF, HALF), cols]
                arrived(ref, recv_s.at[lane * 8 + h])

    def cell(h, t):
        o, half = ORDER[h]
        f0, fn = F_TILES[t]
        if t == 0:
            half_ready(h)
        if h == FIRST:
            arrived(w2.at[1 - xl, pl.ds(f0, fn), :], recv_w.at[t])
        rows = pl.ds(half * HALF, HALF)
        tile = product(lax.rem(y + o, 4), half, f0, fn)
        part[o - 1, half * HALF : (half + 1) * HALF, f0 : f0 + fn] = tile.astype(jnp.bfloat16)
        src = part.at[o - 1, rows, pl.ds(f0, fn)]
        dst = got.at[o - 1, rows, pl.ds(f0, fn)]
        rsem = recv_r.at[(2 * (o - 1) + half) * 4 + t]
        remote(src, dst, send_r.at[o - 1], rsem, (ring_y(o), c)).start()

    def pass_on():
        arrived(ht.at[slot_p], recv_h.at[slot_p])
        to_neighbours(slot_p, (0, OVER_Y))

    def opposite_hidden(kind, base):
        slot = lax.rem(base + 4, 8)
        arrived(ht.at[slot, pl.ds(*(UP, UP2)[kind]), :], recv_u.at[kind])
        arrived(ht.at[slot, pl.ds(*(DOWN, DOWN2)[kind]), :], recv_d.at[kind])
        if kind == 0:
            over_x(slot, 2)

    def extra_ready(o):
        yb = lax.rem(y + o, 4)
        for h in range(8):
            if ORDER[h][0] == o:
                for way in range(2):
                    cols = pl.ds(pl.multiple_of((2 * way + 1 - k) * DC, DC), DC)
                    ref = g2.at[yb, pl.ds(ORDER[h][1] * HALF, HALF), cols]
                    arrived(ref, recv_p.at[way * 8 + h])

    def weight_pass(blocks, first=False, last=False):
        def tile(i, carry):
            cols = pl.ds(pl.multiple_of(i * 256, 256), 256)
            total = None if first else gwv[:, cols]
            for kind, o in blocks:
                yb = lax.rem(y + o, 4)
                left = ht[2 * yb + (xl if kind == 0 else 1 - xl)]
                right = g1[xl, yb, :, cols] if kind == 0 else g2[yb, :, cols]
                term = jnp.dot(left, right, preferred_element_type=jnp.float32)
                total = term if total is None else total + term
            gwv[:, cols] = total
            return carry

        lax.fori_loop(0, DR // 256, tile, 0)

    def own_weights():
        half_ready(0)
        half_ready(1)
        weight_pass([(0, 0)], first=True)

    def opposite_weights():
        opposite_hidden(0, r)
        weight_pass([(0, 2)])

    def extra_weights():
        extra_ready(0)
        weight_pass([(1, 0)])

    base = SKEW * HOPS
    ready = [base + HQ * (h + 1) for h in range(8)]
    events = [
        (AT_PASS, pass_on),
        (AT_OWN, lambda: relay_hidden(0, r)),
        (AT_PARTNER, lambda: relay_hidden(1, slot_p)),
        (ready[1] + 2, own_weights),
        (ready[2] + 3, extra_weights),
        (ready[4] + 3, opposite_weights),
    ]
    for h in range(FIRST, 8):
        for t in range(4):
            step = max(ready[h] + 1 + t // 2, W_AT[t])
            events.append((step, functools.partial(cell, h, t)))
    events.append((NQ + base + LATER, lambda: None))
    load_w.wait()
    at = 0
    for step, event in sorted(events, key=lambda e: e[0]):
        if step > at:
            lax.fori_loop(at, step, z_step, 0)
        event()
        at = step

    for half in range(2):
        for f0, fn in F_TILES:
            acc[half * HALF : (half + 1) * HALF, f0 : f0 + fn] = product(y, half, f0, fn)
    for o in range(1, 4):
        extra_ready(o)
    opposite_hidden(1, slot_p)
    for i, o in enumerate((3, 1, 2)):
        slot = lax.rem(slot_p + 2 * o, 8)
        arrived(ht.at[slot, pl.ds(*OVER_X), :], recv_x.at[i])
    weight_pass([(0, 1), (0, 3), (1, 1), (1, 2), (1, 3)], last=True)

    for i in range(3):
        for half in range(2):
            for t, (f0, fn) in enumerate(F_TILES):
                ref = got.at[i, pl.ds(half * HALF, HALF), pl.ds(f0, fn)]
                arrived(ref, recv_r.at[(2 * i + half) * 4 + t])

    def final_tile(i, carry):
        rows = pl.ds(pl.multiple_of(i * 32, 32), 32)
        gv = ga[rows, :].astype(jnp.float32)
        uv = up[rows, :].astype(jnp.float32)
        gh = acc[rows, :]
        for n in range(3):
            gh = gh + got[n, rows, :].astype(jnp.float32)
        s = jax.nn.sigmoid(gv)
        ggv[rows, :] = (gh * uv * s * (1.0 + gv * (1.0 - s))).astype(jnp.bfloat16)
        guv[rows, :] = (gh * (gv * s)).astype(jnp.bfloat16)
        return carry

    lax.fori_loop(0, TB // 32, final_tile, 0)
    @pl.when(yr != y)
    def _():
        arrived(g_hbm, send_a.at[0])

    arrived(g_hbm, send_a.at[1])
    for d in h_sends + w_sends:
        d.wait_send()
    for i in range(3):
        arrived(part.at[i], send_r.at[i])
    for zb in range(2):
        for way in range(2):
            lane = 2 * zb + way
            whole = g1.at[zb, :, :, lane_cols(way)]

            @pl.when(lane_distance(zb, way) < HOPS)
            def _(whole=whole, lane=lane):
                arrived(whole, send_z.at[lane])

            arrived(whole, send_s.at[lane])
    for way in range(2):
        whole = g2.at[:, :, lane_cols(way)]
        arrived(whole, send_o.at[way])
        arrived(whole, send_p.at[way])


def on_device(grad_out, gate_act, up_act, down_weight):
    bf, f32 = jnp.bfloat16, jnp.float32
    dma = pltpu.SemaphoreType.DMA
    hbm = pl.BlockSpec(memory_space=pltpu.HBM)
    return pl.pallas_call(
        kernel,
        out_shape=(
            pltpu.VMEM((TB, FB), bf),
            pltpu.VMEM((TB, FB), bf),
            pltpu.VMEM((FB, DR), f32),
        ),
        in_specs=[hbm] * 4,
        out_specs=(pl.BlockSpec(memory_space=pltpu.VMEM),) * 3,
        scratch_shapes=[
            pltpu.VMEM((2, 4, TB, DR), bf),
            pltpu.VMEM((4, TB, DR), bf),
            pltpu.VMEM((2, FB, DR), bf),
            pltpu.VMEM((8, FB, TB), bf),
            pltpu.VMEM((3, TB, FB), bf),
            pltpu.VMEM((3, TB, FB), bf),
            pltpu.VMEM((TB, FB), f32),
            pltpu.VMEM((TB, FB), bf),
            pltpu.VMEM((TB, FB), bf),
            dma((3,)),
            dma((2,)), dma((8 * AP,)), dma((4,)), dma((4,)), dma((12,)), dma((8,)), dma((2,)), dma((2,)), dma((3,)),
            dma((3,)), dma((24,)),
            dma((4,)), dma((4 * NQ,)), dma((4,)), dma((32,)),
            dma((2,)), dma((2 * NQ,)), dma((2,)), dma((16,)),
        ],
        compiler_params=pltpu.CompilerParams(
            collective_id=0, has_side_effects=True, vmem_limit_bytes=59 * 1024 * 1024
        ),
    )(grad_out, gate_act, up_act, down_weight)


def solution(mesh):
    placed = (P("row", "col"), P("row", "col"), P("row", "col"), P("col", "row"))
    return jax.shard_map(
        on_device,
        mesh=mesh,
        in_specs=placed,
        out_specs=(P("row", "col"), P("row", "col"), P("col", "row")),
        check_vma=False,
    )
```
